32 devices in a mesh: dp: 8 (over y, x, core), tensor: 4 (over z).
Axes of the slice: x: 2, y: 2, z: 4, core: 2. Of those that a mesh axis runs over, the one named last changes fastest.
Arguments:
- tokens: bfloat16 [2, 8192, 1536], P(None, ('dp', 'tensor')), may hold values from -6 to 6
- cotangent: bfloat16 [2, 8192, 1536], P(None, ('dp', 'tensor')), may hold values from -6 to 6
- segment_ids: int32 [2, 8192], P(None, 'dp'), may hold values from 0 to 1, as said below
- slot_mask: int32 [2, 8192], P(None, 'dp'), may hold values from 0 to 1, as said below
- attention_gain: float32 [1536], replicated, may hold values from 0.5 to 1.5
- query_weight: bfloat16 [1536, 1536], P('dp', 'tensor'), may hold values from -0.15625 to 0.15625
- key_weight: bfloat16 [1536, 1536], P('dp', 'tensor'), may hold values from -0.15625 to 0.15625
- value_weight: bfloat16 [1536, 1536], P('dp', 'tensor'), may hold values from -0.15625 to 0.15625
- forget_weight: bfloat16 [1536, 24], P('dp', 'tensor'), may hold values from -0.15625 to 0.15625
- forget_bias: float32 [24], replicated, may hold values from 1 to 8
- output_weight: bfloat16 [1536, 1536], P(('tensor', 'dp')), may hold values from -0.625 to 0.625
- swiglu_gain: float32 [1536], replicated, may hold values from 0.5 to 1.5
- gate_weight: bfloat16 [1536, 4096], P('dp', 'tensor'), may hold values from -0.15625 to 0.15625
- up_weight: bfloat16 [1536, 4096], P('dp', 'tensor'), may hold values from -0.15625 to 0.15625
- down_weight: bfloat16 [4096, 1536], P(('tensor', 'dp')), may hold values from -0.1875 to 0.1875
Outputs:
- layer_out: bfloat16 [2, 8192, 1536], P(None, ('dp', 'tensor'))
- grad_tokens: float32 [2, 8192, 1536], P(None, ('dp', 'tensor'))
- grad_attention_gain: float32 [1536], replicated
- grad_query: float32 [1536, 1536], P('dp', 'tensor')
- grad_key: float32 [1536, 1536], P('dp', 'tensor')
- grad_value: float32 [1536, 1536], P('dp', 'tensor')
- grad_forget: float32 [1536, 24], P('dp', 'tensor')
- grad_forget_bias: float32 [24], replicated
- grad_output: float32 [1536, 1536], P(('tensor', 'dp'))
- grad_swiglu_gain: float32 [1536], replicated
- grad_gate: float32 [1536, 4096], P('dp', 'tensor')
- grad_up: float32 [1536, 4096], P('dp', 'tensor')
- grad_down: float32 [4096, 1536], P(('tensor', 'dp'))
The draws below stay inside these ranges and needn't reach their ends.
Inputs may be any that keep to these rules, and one draw needn't show every extreme that they name: `segment_ids`: within each aligned block of 1024 slots the ids start at 0 and never fall, and a block holds at most 2 sequences; every sequence lies in one block; the first block of every micro-batch holds one sequence. `slot_mask`: padding slots stand at the end of an aligned block of 1024 slots.
All inputs are finite; a program needn't handle non-finite values.
Results may differ from the reference program's by a relative error of at most 0.019.
Values may be sent and summed in bfloat16 or wider, within the bound.
No kernel may reach another device: no remote copies, remote signals or barrier semaphores. Data moves between devices by JAX's collectives and lax.ppermute only.
A program may use at most 168 MiB of HBM per device.

```python
import math
import jax
import jax.numpy as jnp
from jax import lax

D = 1536
H = 24
DH = 64
FF = 4096
TOK_DP = 1024
MB = 2
TOKENS = 8192


def draw_segment_ids(key, part):
    blocks = TOKENS // TOK_DP
    split = jax.random.randint(key, (MB, blocks, 1), TOK_DP // 4, 3 * TOK_DP // 4 + 1)
    places = jnp.arange(TOK_DP, dtype=jnp.int32)[None, None, :]
    block_index = jnp.arange(blocks, dtype=jnp.int32)[None, :, None]
    later = (places >= split) & (block_index > 0)
    ids = later.astype(jnp.int32)
    return ids.reshape(MB, TOKENS).astype(jnp.int32)


def draw_slot_mask(key, part):
    blocks = TOKENS // TOK_DP
    padding = jax.random.randint(jax.random.fold_in(key, 7), (MB, blocks, 1), 0, TOK_DP // 8 + 1)
    places = jnp.arange(TOK_DP, dtype=jnp.int32)[None, None, :]
    present = (places < TOK_DP - padding).astype(jnp.int32)
    return present.reshape(MB, TOKENS)


def shard_levels(key, dims, shards, smallest, largest):
    def one(position, shards_of):
        draws = jax.random.uniform(jax.random.fold_in(jax.random.fold_in(key, 6), position), (shards_of,), jnp.float32, smallest / len(shards), largest / len(shards))
        return jnp.repeat(jnp.exp(draws), dims[position] // shards_of).reshape((-1,) + (1,) * (len(dims) - position - 1))

    level = one(*shards[0])
    for cut in shards[1:]:
        level = level * one(*cut)
    return level


def gaussian(key, dims, width, bound, cuts=(), kind=jnp.bfloat16):
    entries = jax.random.normal(key, dims, jnp.float32) * width
    if len(cuts) > 0:
        entries = shard_levels(key, dims, cuts, -0.22, 0.18) * entries
    return jnp.clip(entries, min=-bound, max=bound).astype(kind)


def setup_inputs(seed: int = 0) -> dict:
    arg_keys = jax.random.split(jax.random.key(seed), 16)
    tokens = gaussian(arg_keys[0], (MB, TOKENS, D), 1.0, 6.0, ((1, 32),))
    cotangent = gaussian(arg_keys[1], (MB, TOKENS, D), 1.0, 6.0, ((1, 32),))
    segment_ids = draw_segment_ids(jax.random.fold_in(arg_keys[15], 71), 0)
    slot_mask = draw_slot_mask(jax.random.fold_in(arg_keys[15], 71), 0)
    attention_gain = jnp.clip(1.0 + 0.1 * jax.random.normal(arg_keys[4], (D,), jnp.float32), 0.5, 1.5)
    query_weight = gaussian(arg_keys[5], (D, H * DH), D ** -0.5, 0.15625, ((0, 8), (1, 4)))
    key_weight = gaussian(arg_keys[6], (D, H * DH), D ** -0.5, 0.15625, ((0, 8), (1, 4)))
    value_weight = gaussian(arg_keys[7], (D, H * DH), D ** -0.5, 0.15625, ((0, 8), (1, 4)))
    forget_weight = gaussian(arg_keys[8], (D, H), D ** -0.5, 0.15625, ((0, 8), (1, 4)))
    forget_bias = jnp.clip(jnp.exp(jax.random.uniform(arg_keys[9], (H,), jnp.float32, math.log(1.0), math.log(8.0))), 1.0, 8.0)
    output_weight = gaussian(arg_keys[10], (H * DH, D), (H * DH // 16) ** -0.5, 0.625, ((0, 32),))
    swiglu_gain = jnp.clip(1.0 + 0.1 * jax.random.normal(arg_keys[11], (D,), jnp.float32), 0.5, 1.5)
    gate_weight = gaussian(arg_keys[12], (D, FF), D ** -0.5, 0.15625, ((0, 8), (1, 4)))
    up_weight = gaussian(arg_keys[13], (D, FF), D ** -0.5, 0.15625, ((0, 8), (1, 4)))
    down_weight = gaussian(arg_keys[14], (FF, D), (FF // 4) ** -0.5, 0.1875, ((0, 32),))
    return dict(tokens=tokens, cotangent=cotangent, segment_ids=segment_ids, slot_mask=slot_mask, attention_gain=attention_gain, query_weight=query_weight, key_weight=key_weight, value_weight=value_weight, forget_weight=forget_weight, forget_bias=forget_bias, output_weight=output_weight, swiglu_gain=swiglu_gain, gate_weight=gate_weight, up_weight=up_weight, down_weight=down_weight)


EPS = 1e-05
HIGH = lax.Precision.HIGHEST

@jax.custom_vjp
def low(v):
    return lax.optimization_barrier(v.astype(jnp.bfloat16)).astype(jnp.float32)

@jax.custom_vjp
def low_back(v):
    return v

def low_keep(v):
    return (low(v), None)

def low_pass(kept, grad):
    return (grad,)

def back_keep(v):
    return (v, None)

def back_low(kept, grad):
    return (low(grad),)
low.defvjp(low_keep, low_pass)
low_back.defvjp(back_keep, back_low)

def matmul(left, right):
    return jnp.dot(left, right, precision=HIGH)

def rms_scale(rows, gain):
    return rows * lax.rsqrt(lax.optimization_barrier(jnp.mean(rows * rows, axis=-1, keepdims=True)) + EPS) * gain

def unit_forward(params, rows, segment, present):
    attention_gain, query_weight, key_weight, value_weight, forget_weight, forget_bias, output_weight, swiglu_gain, gate_weight, up_weight, down_weight = params
    length = rows.shape[0]
    normed = low(rms_scale(rows, attention_gain))
    queries = low(low_back(matmul(normed, query_weight))).reshape(length, H, DH)
    keys_all = low(low_back(matmul(normed, key_weight))).reshape(length, H, DH)
    values_all = low(low_back(matmul(normed, value_weight))).reshape(length, H, DH)
    logits = low_back(matmul(normed, forget_weight) + forget_bias)
    decay = jnp.cumsum(jax.nn.log_sigmoid(logits), axis=0).T
    scores = jnp.einsum('qhd,khd->hqk', queries, keys_all, precision=HIGH) * DH ** (-0.5)
    scores = low_back(scores + decay[:, :, None] - decay[:, None, :])
    places = jnp.arange(length, dtype=jnp.int32)
    allowed = (places[None, :] <= places[:, None]) & (segment[:, None] == segment[None, :])
    allowed = allowed & ((present[None, :] == 1) | (places[None, :] == places[:, None]))
    scores = jnp.where(allowed[None], scores, -1e+30)
    probs = jax.nn.softmax(scores, axis=-1)
    mixed = jnp.einsum('hqk,khd->qhd', low(probs), values_all, precision=HIGH).reshape(length, H * DH)
    mixed = low_back(low(mixed))
    hidden_state = rows + low_back(matmul(mixed, output_weight))
    normed_two = low(rms_scale(hidden_state, swiglu_gain))
    gate = low_back(matmul(normed_two, gate_weight))
    upper = low_back(matmul(normed_two, up_weight))
    inner = low(jax.nn.silu(gate) * upper)
    return hidden_state + low_back(matmul(inner, down_weight))

def reference(tokens, cotangent, segment_ids, slot_mask, attention_gain, query_weight, key_weight, value_weight, forget_weight, forget_bias, output_weight, swiglu_gain, gate_weight, up_weight, down_weight):
    params = tuple((item.astype(jnp.float32) for item in (attention_gain, query_weight, key_weight, value_weight, forget_weight, forget_bias, output_weight, swiglu_gain, gate_weight, up_weight, down_weight)))
    units = MB * (TOKENS // TOK_DP)
    segments = segment_ids.reshape(units, TOK_DP)
    presence = slot_mask.reshape(units, TOK_DP)

    def forward(token_rows, weights):
        blocks = token_rows.reshape(units, TOK_DP, D)
        step = jax.checkpoint(lambda item: unit_forward(weights, item[0], item[1], item[2]))
        result = lax.map(step, (blocks, segments, presence))
        return result.reshape(MB, TOKENS, D)
    output, pullback = jax.vjp(forward, tokens.astype(jnp.float32), params)
    grad_rows, grads = pullback(cotangent.astype(jnp.float32))
    g_attention_gain, g_query, g_key, g_value, g_forget, g_forget_bias, g_output, g_swiglu_gain, g_gate, g_up, g_down = grads
    return (output.astype(jnp.bfloat16), grad_rows, g_attention_gain, g_query, g_key, g_value, g_forget, g_forget_bias, g_output, g_swiglu_gain, g_gate, g_up, g_down)
```

```python
import jax
import jax.numpy as jnp
from jax import lax
from jax.sharding import PartitionSpec as P

EPS = 1e-05
NEGATIVE = -1e30
F32 = jnp.float32
BF16 = jnp.bfloat16


def rms_forward(rows, gain):
    inverse = lax.rsqrt(jnp.mean(rows * rows, axis=-1, keepdims=True) + EPS)
    return (rows * inverse * gain, inverse)


def rms_backward(rows, inverse, gain, upstream):
    scaled = upstream * gain
    return inverse * scaled - rows * inverse**3 * jnp.mean(scaled * rows, axis=-1, keepdims=True)


def dot(left, right, left_dim, right_dim):
    return lax.dot_general(
        left, right, (((left_dim,), (right_dim,)), ((), ())), preferred_element_type=F32
    )


def allowed_block(segment, present, first, size):
    length = segment.shape[0]
    places = jnp.arange(length, dtype=jnp.int32)
    query_places = first + jnp.arange(size, dtype=jnp.int32)
    query_segment = segment[first : first + size]
    allowed = (places[None, :] <= query_places[:, None]) & (
        query_segment[:, None] == segment[None, :]
    )
    return allowed & ((present[None, :] == 1) | (places[None, :] == query_places[:, None]))


def block_scores(query_block, keys_all, decay, first, size, allowed, scale):
    raw = (
        jnp.einsum("qhd,khd->hqk", query_block, keys_all, preferred_element_type=F32) * scale
    )
    raw = raw + decay[:, first : first + size, None] - decay[:, None, :]
    return jnp.where(allowed[None], raw, NEGATIVE)


def attention_forward(queries, keys_all, values_all, decay, segment, present):
    length = queries.shape[0]
    scale = queries.shape[2] ** (-0.5)
    block = min(512, length)
    mixed_blocks = []
    total_blocks = []
    for first in range(0, length, block):
        allowed = allowed_block(segment, present, first, block)
        scores = block_scores(
            queries[first : first + block], keys_all, decay, first, block, allowed, scale
        )
        highest = jnp.max(scores, axis=-1, keepdims=True)
        expo = jnp.exp(scores - highest)
        denominator = jnp.sum(expo, axis=-1, keepdims=True)
        probs = (expo / denominator).astype(BF16)
        mixed_blocks.append(
            jnp.einsum("hqk,khd->qhd", probs, values_all, preferred_element_type=F32).astype(BF16)
        )
        total_blocks.append((highest + jnp.log(denominator))[:, :, 0])
    return (jnp.concatenate(mixed_blocks, axis=0), jnp.concatenate(total_blocks, axis=1))


def attention_backward(
    queries, keys_all, values_all, decay, log_total, grad_mixed, segment, present
):
    length = queries.shape[0]
    scale = queries.shape[2] ** (-0.5)
    block = min(512, length)
    grad_keys = jnp.zeros(keys_all.shape, F32)
    grad_values = jnp.zeros(values_all.shape, F32)
    grad_decay = jnp.zeros(decay.shape, F32)
    query_grads = []
    for first in range(0, length, block):
        allowed = allowed_block(segment, present, first, block)
        query_block = queries[first : first + block]
        grad_block = grad_mixed[first : first + block]
        scores = block_scores(query_block, keys_all, decay, first, block, allowed, scale)
        probs = jnp.exp(scores - log_total[:, first : first + block, None])
        grad_values = grad_values + jnp.einsum(
            "hqk,qhd->khd", probs.astype(BF16), grad_block, preferred_element_type=F32
        )
        grad_probs = jnp.einsum("qhd,khd->hqk", grad_block, values_all, preferred_element_type=F32)
        grad_scores = probs * (grad_probs - jnp.sum(probs * grad_probs, axis=-1, keepdims=True))
        grad_low = grad_scores.astype(BF16)
        query_grads.append(
            (
                jnp.einsum("hqk,khd->qhd", grad_low, keys_all, preferred_element_type=F32) * scale
            ).astype(BF16)
        )
        grad_keys = (
            grad_keys
            + jnp.einsum("hqk,qhd->khd", grad_low, query_block, preferred_element_type=F32) * scale
        )
        as_float = grad_low.astype(F32)
        grad_decay = grad_decay.at[:, first : first + block].add(jnp.sum(as_float, axis=-1))
        grad_decay = grad_decay - jnp.sum(as_float, axis=1)
    return (
        jnp.concatenate(query_grads, axis=0),
        grad_keys.astype(BF16),
        grad_values.astype(BF16),
        grad_decay,
    )


def after(value, *others):
    return lax.optimization_barrier((value,) + others)[0]


def body(
    tokens,
    cotangent,
    segment_ids,
    slot_mask,
    attention_gain,
    query_weight,
    key_weight,
    value_weight,
    forget_weight,
    forget_bias,
    output_weight,
    swiglu_gain,
    gate_weight,
    up_weight,
    down_weight,
):
    batches, here, width = tokens.shape
    ranks = lax.axis_size("tensor")
    groups = lax.axis_size("dp")
    length = here * ranks
    heads_here = forget_weight.shape[1]
    head_width = query_weight.shape[1]
    head_size = head_width // heads_here
    units_here = gate_weight.shape[1]
    units = units_here * ranks
    unit_piece = down_weight.shape[0]
    head_piece = output_weight.shape[0]
    rank = lax.axis_index("tensor")
    bias_here = lax.dynamic_slice_in_dim(forget_bias, rank * heads_here, heads_here)

    def shift(value, step):
        if step % ranks == 0:
            return value
        return lax.ppermute(value, "tensor", [(i, (i + step) % ranks) for i in range(ranks)])

    def pieces_of(value):
        return [shift(value, step) for step in range(ranks)]

    def row_block(value, owner):
        return lax.dynamic_slice_in_dim(value, (owner % ranks) * here, here, 0)

    def place_rows(blocks, owners):
        total = jnp.zeros((length,) + blocks[0].shape[1:], blocks[0].dtype)
        for block, owner in zip(blocks, owners):
            total = lax.dynamic_update_slice_in_dim(total, block, (owner % ranks) * here, 0)
        return total

    mixed_in = jnp.concatenate((query_weight, key_weight, value_weight, forget_weight), axis=1)
    full_in = lax.all_gather(mixed_in, "dp", axis=0, tiled=True)
    output_pieces = pieces_of(output_weight)
    full_output = lax.all_gather(jnp.stack(output_pieces), "dp", axis=0)
    full_output = full_output.transpose(1, 0, 2, 3).reshape(ranks * head_width, width)
    pair = jnp.concatenate((gate_weight, up_weight), axis=1)
    pair_pieces = pieces_of(after(pair, *output_pieces))

    def by_unit(blocks):
        split = [block.reshape(block.shape[0], groups, unit_piece) for block in blocks]
        return jnp.stack(split, axis=2).reshape(blocks[0].shape[0], units)

    pair_rows = jnp.concatenate(
        (
            by_unit([piece[:, :units_here] for piece in pair_pieces]),
            by_unit([piece[:, units_here:] for piece in pair_pieces]),
        ),
        axis=1,
    )
    full_pair = lax.all_gather(pair_rows, "dp", axis=0, tiled=True)

    rows = tokens.astype(F32)
    normed, inverse_one = rms_forward(rows, attention_gain)
    normed = normed.astype(BF16)
    saved = []
    mixed_parts = []
    previous = pair_pieces
    for batch in range(batches):
        normed_pieces = pieces_of(after(normed[batch], *previous))
        previous = normed_pieces
        normed_all = place_rows(normed_pieces, [rank - step + ranks for step in range(ranks)])
        projected = dot(normed_all, full_in, 1, 0)
        queries = projected[:, :head_width].astype(BF16).reshape(length, heads_here, head_size)
        keys_all = (
            projected[:, head_width : 2 * head_width]
            .astype(BF16)
            .reshape(length, heads_here, head_size)
        )
        values_all = (
            projected[:, 2 * head_width : 3 * head_width]
            .astype(BF16)
            .reshape(length, heads_here, head_size)
        )
        logits = projected[:, 3 * head_width :] + bias_here
        decay = jnp.cumsum(jax.nn.log_sigmoid(logits), axis=0).T
        mixed, log_total = attention_forward(
            queries, keys_all, values_all, decay, segment_ids[batch], slot_mask[batch]
        )
        mixed_flat = mixed.reshape(length, head_width)
        mixed_parts.append(
            jnp.concatenate(
                [shift(row_block(mixed_flat, rank + step), step) for step in range(ranks)], axis=1
            )
        )
        saved.append((normed_all, queries, keys_all, values_all, logits, decay, log_total))
    down_pieces = pieces_of(after(down_weight, *previous))
    full_down = lax.all_gather(jnp.concatenate(down_pieces, axis=0), "dp", axis=0, tiled=True)

    mixed_here = jnp.concatenate(mixed_parts, axis=0)
    rows = rows.reshape(batches * here, width)
    upstream = cotangent.reshape(batches * here, width)
    hidden_state = rows + dot(mixed_here, full_output, 1, 0)
    normed_two, inverse_two = rms_forward(hidden_state, swiglu_gain)
    normed_two = normed_two.astype(BF16)
    both = dot(normed_two, full_pair, 1, 0)
    gate, upper = both[:, :units], both[:, units:]
    sigmoid_gate = jax.nn.sigmoid(gate)
    inner = (gate * sigmoid_gate * upper).astype(BF16)
    layer_out = (hidden_state + dot(inner, full_down, 1, 0)).astype(BF16)

    grad_inner = dot(upstream, full_down, 1, 1)
    grad_both = jnp.concatenate(
        (
            (grad_inner * upper * sigmoid_gate * (1.0 + gate * (1.0 - sigmoid_gate))).astype(BF16),
            (grad_inner * gate * sigmoid_gate).astype(BF16),
        ),
        axis=1,
    )

    def scatter(value):
        return lax.psum_scatter(value, "dp", scatter_dimension=0, tiled=True)

    def settle(blocks):
        total = blocks[0].astype(F32)
        for step in range(1, ranks):
            total = total + shift(blocks[step], ranks - step).astype(F32)
        return total

    down_rows = scatter(dot(inner, upstream, 0, 0).astype(BF16))
    pair_grad = scatter(dot(normed_two, grad_both, 0, 0).astype(BF16))
    grad_normed_two = dot(grad_both, full_pair, 1, 1)
    gain_two = jnp.sum(grad_normed_two * hidden_state * inverse_two, axis=0)
    grad_hidden = upstream.astype(F32) + rms_backward(
        hidden_state, inverse_two, swiglu_gain, grad_normed_two
    )
    branch = grad_hidden.astype(BF16)
    output_rows = dot(mixed_here, branch, 0, 0).astype(BF16)
    output_rows = output_rows.reshape(ranks, groups, head_piece, width).transpose(1, 0, 2, 3)
    output_rows = scatter(output_rows.reshape(ranks * head_width, width))
    grad_mixed_here = dot(branch, full_output, 1, 1).astype(BF16)

    projected_grads = []
    bias_grad = jnp.zeros((heads_here,), F32)
    gain_one = jnp.zeros((width,), F32)
    grad_tokens = []
    for batch in range(batches):
        normed_all, queries, keys_all, values_all, logits, decay, log_total = saved[batch]
        part = grad_mixed_here[batch * here : (batch + 1) * here]
        blocks = [
            shift(part[:, step * head_width : (step + 1) * head_width], ranks - step)
            for step in range(ranks)
        ]
        grad_mixed = place_rows(blocks, [rank + step for step in range(ranks)])
        late_queries, late_decay, grad_mixed = lax.optimization_barrier(
            (queries, decay, grad_mixed)
        )
        grad_queries, grad_keys, grad_values, grad_decay = attention_backward(
            late_queries,
            keys_all,
            values_all,
            late_decay,
            log_total,
            grad_mixed.reshape(queries.shape),
            segment_ids[batch],
            slot_mask[batch],
        )
        carried = jnp.flip(jnp.cumsum(jnp.flip(grad_decay.T, 0), axis=0), 0)
        grad_logits = (carried * jax.nn.sigmoid(-logits)).astype(BF16)
        projected_grad = jnp.concatenate(
            (
                grad_queries.reshape(length, -1),
                grad_keys.reshape(length, -1),
                grad_values.reshape(length, -1),
                grad_logits,
            ),
            axis=1,
        )
        projected_grads.append(projected_grad)
        bias_grad = bias_grad + jnp.sum(grad_logits.astype(F32), axis=0)
        partial = dot(projected_grad, full_in, 1, 1).astype(BF16)
        grad_normed = row_block(partial, rank).astype(F32)
        for step in range(1, ranks):
            grad_normed = grad_normed + shift(row_block(partial, rank + step), step).astype(F32)
        own = rows[batch * here : (batch + 1) * here]
        gain_one = gain_one + jnp.sum(grad_normed * own * inverse_one[batch], axis=0)
        grad_tokens.append(
            grad_hidden[batch * here : (batch + 1) * here]
            + rms_backward(own, inverse_one[batch], attention_gain, grad_normed)
        )
    in_grad = scatter(
        dot(
            jnp.concatenate([item[0] for item in saved], axis=0),
            jnp.concatenate(projected_grads, axis=0),
            0,
            0,
        ).astype(BF16)
    ).astype(F32)

    down_rows = down_rows.reshape(ranks, unit_piece, width)
    down_grad = settle([down_rows[step] for step in range(ranks)])
    output_rows = output_rows.reshape(ranks, head_piece, width)
    output_grad = settle([output_rows[step] for step in range(ranks)])
    split = pair_grad.reshape(pair_grad.shape[0], 2, groups, ranks, unit_piece)
    pair_grad = settle(
        [split[:, :, :, step].reshape(pair_grad.shape[0], 2 * units_here) for step in range(ranks)]
    )
    bias_full = lax.dynamic_update_slice_in_dim(
        jnp.zeros(forget_bias.shape, F32), bias_grad, rank * heads_here, 0
    )
    gain_one, gain_two, bias_full = lax.psum((gain_one, gain_two, bias_full), ("dp", "tensor"))
    return (
        layer_out.reshape(batches, here, width),
        jnp.stack(grad_tokens),
        gain_one,
        in_grad[:, :head_width],
        in_grad[:, head_width : 2 * head_width],
        in_grad[:, 2 * head_width : 3 * head_width],
        in_grad[:, 3 * head_width :],
        bias_full,
        output_grad,
        gain_two,
        pair_grad[:, :units_here],
        pair_grad[:, units_here:],
        down_grad,
    )


def solution(mesh):
    by_token = P(None, ("dp", "tensor"), None)
    by_column = P("dp", "tensor")
    by_row = P(("tensor", "dp"), None)
    weights = (by_column, by_column, by_column, by_column)
    return jax.shard_map(
        body,
        mesh=mesh,
        in_specs=(by_token, by_token, P(None, "dp"), P(None, "dp"), P())
        + weights
        + (P(), by_row, P(), by_column, by_column, by_row),
        out_specs=(by_token, by_token, P())
        + weights
        + (P(), by_row, P(), by_column, by_column, by_row),
        check_vma=False,
    )
```

```python
import functools
import jax
import jax.numpy as jnp
from jax import lax
from jax.experimental import pallas as pl
from jax.experimental.pallas import tpu as pltpu
from jax.sharding import PartitionSpec as P

EPS = 1e-05
F32 = jnp.float32
BF16 = jnp.bfloat16
LANES = 128
TILE = 256
BIG = 2.0**100


def three_parts(value):
    high = value.astype(BF16).astype(F32)
    rest = value - high
    middle = rest.astype(BF16).astype(F32)
    return high, middle, rest - middle


def lane_pick(array, lane, index):
    return jnp.sum(jnp.where(lane == index, array, 0.0), axis=1, keepdims=True)


def with_extras(data, keep, place, extras):
    total = jnp.where(keep, data, 0.0)
    for index, extra in enumerate(extras):
        total = jnp.where(place == index, extra, total)
    return total.astype(BF16)


def nt(left, right):
    return lax.dot_general(left, right, (((1,), (1,)), ((), ())), preferred_element_type=F32)


def nn(left, right):
    return lax.dot_general(left, right, (((1,), (0,)), ((), ())), preferred_element_type=F32)


def head_sides(head, heads, size, side_ref):
    length = side_ref.shape[0]
    lane = lax.broadcasted_iota(jnp.int32, (length, LANES), 1)
    half = lax.rem(head, 2)
    keep = (lane >= half * size) & (lane < (half + 1) * size)
    place = lane - (1 - half) * size
    place = jnp.where(keep, -1, place)
    side = side_ref[...]
    decay = lane_pick(side, lane, head)
    segment = side[:, heads : heads + 1]
    padded = 1.0 - side[:, heads + 1 : heads + 2]
    return lane, keep, place, decay, segment, padded


def key_extras(decay, segment, padded):
    high, middle, low = three_parts(-decay)
    return [high, middle, low, segment, 1.0 - segment, padded, 1.0, 1.0, 1.0]


def query_extras(segment, total):
    return [1.0, 1.0, 1.0, -BIG * (1.0 - segment), -BIG * segment, -BIG] + list(
        three_parts(-total)
    )


PADDED_AT = 5


def forward_kernel(heads, size, scale, q_ref, k_ref, v_ref, side_ref, o_ref, total_ref, ks_ref):
    head = pl.program_id(0)
    length = q_ref.shape[0]
    lane, keep, place, decay, segment, padded = head_sides(head, heads, size, side_ref)
    ks_ref[...] = with_extras(k_ref[...].astype(F32), keep, place, key_extras(decay, segment, padded))

    @pl.when(head == 0)
    def _():
        total_ref[...] = jnp.zeros_like(total_ref)

    row = lax.broadcasted_iota(jnp.int32, (TILE, TILE), 0)
    column = lax.broadcasted_iota(jnp.int32, (TILE, TILE), 1)
    for first in range(0, length, TILE):
        here = pl.ds(first, TILE)
        part = slice(first, first + TILE)
        full = with_extras(
            q_ref[here, :].astype(F32) * scale, keep[part], place[part],
            query_extras(segment[part], 0.0 * segment[part]),
        )
        bare = jnp.where(place[part] == PADDED_AT, 0.0, full.astype(F32)).astype(BF16)
        keys = ks_ref[here, :]
        near = jnp.where(
            column < row, nt(full, keys), jnp.where(column == row, nt(bare, keys), -BIG)
        )
        highest = jnp.max(near, axis=1, keepdims=True)
        if first:
            far = nt(full, ks_ref[pl.ds(0, first), :])
            highest = jnp.maximum(highest, jnp.max(far, axis=1, keepdims=True))
        near = jnp.exp(near - highest)
        below = jnp.sum(near, axis=1, keepdims=True)
        mixed = nn(near.astype(BF16), v_ref[here, :])
        if first:
            far = jnp.exp(far - highest)
            below = below + jnp.sum(far, axis=1, keepdims=True)
            mixed = mixed + nn(far.astype(BF16), v_ref[pl.ds(0, first), :])
        mixed = (mixed / below).astype(BF16)
        o_ref[here, :] = jnp.where(keep[part], mixed, o_ref[here, :])
        total_ref[here, :] = jnp.where(
            lane[part] == head, highest + jnp.log(below), total_ref[here, :]
        )


def backward_kernel(
    heads, size, scale, q_ref, k_ref, v_ref, side_ref, total_ref, o_ref, g_ref,
    dq_ref, dk_ref, dv_ref, dd_ref, ks_ref, kt_ref, vs_ref, ak_ref, av_ref, row_ref,
):
    head = pl.program_id(0)
    length = q_ref.shape[0]
    lane, keep, place, decay, segment, padded = head_sides(head, heads, size, side_ref)
    keys = with_extras(k_ref[...].astype(F32), keep, place, key_extras(decay, segment, padded))
    ks_ref[...] = keys
    kt_ref[...] = keys.astype(F32).T.astype(BF16)
    vs_ref[...] = with_extras(v_ref[...].astype(F32), keep, place, [1.0, 1.0, 1.0])
    total = lane_pick(total_ref[...], lane, head)
    grads = jnp.where(keep, g_ref[...].astype(F32), 0.0)
    delta = jnp.sum(grads * o_ref[...].astype(F32), axis=1, keepdims=True)
    ak_ref[...] = jnp.zeros_like(ak_ref)
    av_ref[...] = jnp.zeros_like(av_ref)

    @pl.when(head == 0)
    def _():
        dd_ref[...] = jnp.zeros_like(dd_ref)

    row = lax.broadcasted_iota(jnp.int32, (TILE, TILE), 0)
    column = lax.broadcasted_iota(jnp.int32, (TILE, TILE), 1)
    for first in range(0, length, TILE):
        here = pl.ds(first, TILE)
        part = slice(first, first + TILE)
        full = with_extras(
            q_ref[here, :].astype(F32) * scale, keep[part], place[part],
            query_extras(segment[part], total[part]),
        )
        bare = jnp.where(place[part] == PADDED_AT, 0.0, full.astype(F32)).astype(BF16)
        grad = with_extras(grads[part], keep[part], place[part], three_parts(-delta[part]))
        spans = [(first, TILE)] + ([(0, first)] if first else [])
        grad_query = None
        for start, count in spans:
            span = pl.ds(start, count)
            scores = nt(ks_ref[span, :], full)
            if start == first:
                scores = jnp.where(
                    row < column, scores, jnp.where(row == column, nt(ks_ref[span, :], bare), -BIG)
                )
            probs = jnp.exp(scores)
            low = (probs * nt(vs_ref[span, :], grad)).astype(BF16)
            av_ref[span, :] += nn(probs.astype(BF16), grad)
            ak_ref[span, :] += nn(low, full)
            piece = nn(kt_ref[:, span], low)
            grad_query = piece if grad_query is None else grad_query + piece
        grad_query = grad_query.T
        dq_ref[here, :] = jnp.where(keep[part], (grad_query * scale).astype(BF16), dq_ref[here, :])
        row_ref[here, :] = grad_query
    dk_ref[...] = jnp.where(keep, ak_ref[...].astype(BF16), dk_ref[...])
    dv_ref[...] = jnp.where(keep, av_ref[...].astype(BF16), dv_ref[...])
    by_row = lane_pick(row_ref[...], place, 6)
    by_column = lane_pick(ak_ref[...], place, 0)
    dd_ref[...] = jnp.where(lane == head, by_row - by_column, dd_ref[...])


def specs_for(length, size, heads):
    def pair(offset):
        return pl.BlockSpec((length, LANES), lambda h: (0, offset * heads * size // LANES + h // 2))

    return pair, pl.BlockSpec((length, LANES), lambda h: (0, 0))


def make_side(decay, segment, present):
    length, heads = decay.shape
    side = jnp.concatenate(
        (decay, segment[:, None].astype(F32), present[:, None].astype(F32)), axis=1
    )
    return jnp.pad(side, ((0, 0), (0, LANES - heads - 2)))


def attention_forward(projected, side, heads, size):
    length = projected.shape[0]
    pair, whole = specs_for(length, size, heads)
    return pl.pallas_call(
        functools.partial(forward_kernel, heads, size, size ** (-0.5)),
        grid=(heads,),
        in_specs=[pair(0), pair(1), pair(2), whole],
        out_specs=[pair(0), whole],
        out_shape=[
            jax.ShapeDtypeStruct((length, heads * size), BF16),
            jax.ShapeDtypeStruct((length, LANES), F32),
        ],
        scratch_shapes=[pltpu.VMEM((length, LANES), BF16)],
    )(projected, projected, projected, side)


def attention_backward(projected, side, total, mixed, grad_mixed, heads, size):
    length = projected.shape[0]
    pair, whole = specs_for(length, size, heads)
    flat = jax.ShapeDtypeStruct((length, heads * size), BF16)
    return pl.pallas_call(
        functools.partial(backward_kernel, heads, size, size ** (-0.5)),
        grid=(heads,),
        in_specs=[pair(0), pair(1), pair(2), whole, whole, pair(0), pair(0)],
        out_specs=[pair(0), pair(0), pair(0), whole],
        out_shape=[flat, flat, flat, jax.ShapeDtypeStruct((length, LANES), F32)],
        scratch_shapes=[
            pltpu.VMEM((length, LANES), BF16),
            pltpu.VMEM((LANES, length), BF16),
            pltpu.VMEM((length, LANES), BF16),
            pltpu.VMEM((length, LANES), F32),
            pltpu.VMEM((length, LANES), F32),
            pltpu.VMEM((length, LANES), F32),
        ],
    )(projected, projected, projected, side, total, mixed, grad_mixed)


def rms_forward(rows, gain):
    inverse = lax.rsqrt(jnp.mean(rows * rows, axis=-1, keepdims=True) + EPS)
    return (rows * inverse * gain, inverse)


def rms_backward(rows, inverse, gain, upstream):
    scaled = upstream * gain
    return inverse * scaled - rows * inverse**3 * jnp.mean(scaled * rows, axis=-1, keepdims=True)


def dot(left, right, left_dim, right_dim):
    return lax.dot_general(
        left, right, (((left_dim,), (right_dim,)), ((), ())), preferred_element_type=F32
    )


def after(value, *others):
    return lax.optimization_barrier((value,) + others)[0]


def sum_everywhere(value, axes):
    for axis in axes:
        size = lax.axis_size(axis)
        if size & (size - 1):
            value = lax.psum(value, axis)
            continue
        step = 1
        while step < size:
            value = value + lax.ppermute(value, axis, [(i, i ^ step) for i in range(size)])
            step *= 2
    return value


def body(
    tokens,
    cotangent,
    segment_ids,
    slot_mask,
    attention_gain,
    query_weight,
    key_weight,
    value_weight,
    forget_weight,
    forget_bias,
    output_weight,
    swiglu_gain,
    gate_weight,
    up_weight,
    down_weight,
):
    batches, here, width = tokens.shape
    ranks = lax.axis_size("tensor")
    groups = lax.axis_size("dp")
    length = here * ranks
    heads_here = forget_weight.shape[1]
    head_width = query_weight.shape[1]
    head_size = head_width // heads_here
    units_here = gate_weight.shape[1]
    units = units_here * ranks
    unit_piece = down_weight.shape[0]
    head_piece = output_weight.shape[0]
    rank = lax.axis_index("tensor")
    bias_here = lax.dynamic_slice_in_dim(forget_bias, rank * heads_here, heads_here)

    def shift(value, step):
        if step % ranks == 0:
            return value
        return lax.ppermute(value, "tensor", [(i, (i + step) % ranks) for i in range(ranks)])

    def pieces_of(value):
        return [shift(value, step) for step in range(ranks)]

    def row_block(value, owner):
        return lax.dynamic_slice_in_dim(value, (owner % ranks) * here, here, 0)

    def place_rows(blocks, owners):
        total = jnp.zeros((length,) + blocks[0].shape[1:], blocks[0].dtype)
        for block, owner in zip(blocks, owners):
            total = lax.dynamic_update_slice_in_dim(total, block, (owner % ranks) * here, 0)
        return total

    mixed_in = jnp.concatenate((query_weight, key_weight, value_weight, forget_weight), axis=1)
    full_in = lax.all_gather(mixed_in, "dp", axis=0, tiled=True)
    row_pieces = pieces_of(jnp.concatenate((output_weight, down_weight), axis=0))
    pair_pieces = pieces_of(
        after(jnp.concatenate((gate_weight, up_weight), axis=1), *row_pieces)
    )
    full_rows = lax.all_gather(jnp.stack(row_pieces), "dp", axis=0)
    full_output = full_rows[:, :, :head_piece].transpose(1, 0, 2, 3)
    full_output = full_output.reshape(ranks * head_width, width)
    full_down = full_rows[:, :, head_piece:].reshape(units, width)

    def by_unit(blocks):
        split = [block.reshape(block.shape[0], groups, unit_piece) for block in blocks]
        return jnp.stack(split, axis=2).reshape(blocks[0].shape[0], units)

    pair_rows = jnp.concatenate(
        (
            by_unit([piece[:, :units_here] for piece in pair_pieces]),
            by_unit([piece[:, units_here:] for piece in pair_pieces]),
        ),
        axis=1,
    )
    full_pair = lax.all_gather(pair_rows, "dp", axis=0, tiled=True)

    rows = tokens.astype(F32)
    normed, inverse_one = rms_forward(rows, attention_gain)
    normed = normed.astype(BF16)
    saved = []
    mixed_parts = []
    previous = pair_pieces
    for batch in range(batches):
        normed_pieces = pieces_of(after(normed[batch], *previous))
        previous = normed_pieces
        normed_all = place_rows(normed_pieces, [rank - step + ranks for step in range(ranks)])
        projected = dot(normed_all, full_in[:, : 3 * head_width], 1, 0).astype(BF16)
        logits = dot(normed_all, full_in[:, 3 * head_width :], 1, 0) + bias_here
        decay = jnp.cumsum(jax.nn.log_sigmoid(logits), axis=0)
        side = make_side(decay, segment_ids[batch], slot_mask[batch])
        mixed, total = attention_forward(projected, side, heads_here, head_size)
        mixed_parts.append(
            jnp.concatenate(
                [shift(row_block(mixed, rank + step), step) for step in range(ranks)], axis=1
            )
        )
        saved.append((normed_all, projected, logits, side, total, mixed))

    mixed_here = jnp.concatenate(mixed_parts, axis=0)
    rows = rows.reshape(batches * here, width)
    upstream = cotangent.reshape(batches * here, width)
    hidden_state = rows + dot(mixed_here, full_output, 1, 0)
    normed_two, inverse_two = rms_forward(hidden_state, swiglu_gain)
    normed_two = normed_two.astype(BF16)
    both = dot(normed_two, full_pair, 1, 0)
    gate, upper = both[:, :units], both[:, units:]
    sigmoid_gate = jax.nn.sigmoid(gate)
    inner = (gate * sigmoid_gate * upper).astype(BF16)

    def scatter(value):
        return lax.psum_scatter(value, "dp", scatter_dimension=0, tiled=True)

    def settle(blocks):
        total = blocks[0].astype(F32)
        for step in range(1, ranks):
            total = total + shift(blocks[step], ranks - step).astype(F32)
        return total

    down_partial = dot(inner, upstream, 0, 0).astype(BF16)
    down_rows = scatter(down_partial)
    upstream_late = after(upstream, down_partial)
    grad_inner = dot(upstream_late, full_down, 1, 1)
    grad_both = jnp.concatenate(
        (
            (grad_inner * upper * sigmoid_gate * (1.0 + gate * (1.0 - sigmoid_gate))).astype(BF16),
            (grad_inner * gate * sigmoid_gate).astype(BF16),
        ),
        axis=1,
    )
    pair_partial = dot(normed_two, grad_both, 0, 0).astype(BF16)
    grad_normed_two = dot(after(grad_both, pair_partial), full_pair, 1, 1)
    gain_two = jnp.sum(grad_normed_two * hidden_state * inverse_two, axis=0)
    grad_hidden = upstream.astype(F32) + rms_backward(
        hidden_state, inverse_two, swiglu_gain, grad_normed_two
    )
    branch = grad_hidden.astype(BF16)
    pair_grad = scatter(after(pair_partial, down_rows, branch))
    grad_mixed_here = dot(branch, full_output, 1, 1).astype(BF16)
    inner_late, branch_late = lax.optimization_barrier((inner, branch, grad_mixed_here))[:2]
    layer_out = (hidden_state + dot(inner_late, full_down, 1, 0)).astype(BF16)
    output_partial = dot(mixed_here, branch_late, 0, 0).astype(BF16)
    output_partial = output_partial.reshape(ranks, groups, head_piece, width)
    output_partial = output_partial.transpose(1, 0, 2, 3).reshape(ranks * head_width, width)

    projected_grads = []
    bias_grad = jnp.zeros((heads_here,), F32)
    gain_one = jnp.zeros((width,), F32)
    grad_tokens = []
    for batch in range(batches):
        normed_all, projected, logits, side, total, mixed = saved[batch]
        part = grad_mixed_here[batch * here : (batch + 1) * here]
        blocks = [
            shift(part[:, step * head_width : (step + 1) * head_width], ranks - step)
            for step in range(ranks)
        ]
        grad_mixed = place_rows(blocks, [rank + step for step in range(ranks)])
        if batch + 1 == batches:
            grad_mixed = after(grad_mixed, down_rows, *projected_grads)
        grad_queries, grad_keys, grad_values, grad_decay = attention_backward(
            projected, side, total, mixed, grad_mixed, heads_here, head_size
        )
        carried = jnp.flip(jnp.cumsum(jnp.flip(grad_decay[:, :heads_here], 0), axis=0), 0)
        grad_logits = (carried * jax.nn.sigmoid(-logits)).astype(BF16)
        projected_grad = jnp.concatenate(
            (grad_queries, grad_keys, grad_values, grad_logits), axis=1
        )
        projected_grads.append(projected_grad)
        bias_grad = bias_grad + jnp.sum(grad_logits.astype(F32), axis=0)
        partial = dot(projected_grad, full_in, 1, 1).astype(BF16)
        grad_normed = row_block(partial, rank).astype(F32)
        for step in range(1, ranks):
            grad_normed = grad_normed + shift(row_block(partial, rank + step), step).astype(F32)
        own = rows[batch * here : (batch + 1) * here]
        gain_one = gain_one + jnp.sum(grad_normed * own * inverse_one[batch], axis=0)
        grad_tokens.append(
            grad_hidden[batch * here : (batch + 1) * here]
            + rms_backward(own, inverse_one[batch], attention_gain, grad_normed)
        )
    in_partial = dot(
        jnp.concatenate([item[0] for item in saved], axis=0),
        jnp.concatenate(projected_grads, axis=0),
        0,
        0,
    ).astype(BF16)
    last = scatter(after(jnp.concatenate((output_partial, in_partial), axis=1), pair_grad))
    in_grad = last[:, width:].astype(F32)

    down_rows = down_rows.reshape(ranks, unit_piece, width)
    down_grad = settle([down_rows[step] for step in range(ranks)])
    split = pair_grad.reshape(pair_grad.shape[0], 2, groups, ranks, unit_piece)
    pair_grad = settle(
        [split[:, :, :, step].reshape(pair_grad.shape[0], 2 * units_here) for step in range(ranks)]
    )
    output_rows = last[:, :width].reshape(ranks, head_piece, width)
    output_grad = settle([output_rows[step] for step in range(ranks)])
    bias_full = lax.dynamic_update_slice_in_dim(
        jnp.zeros(forget_bias.shape, F32), bias_grad, rank * heads_here, 0
    )
    sums = sum_everywhere(jnp.concatenate((gain_one, gain_two, bias_full)), ("dp", "tensor"))
    return (
        layer_out.reshape(batches, here, width),
        jnp.stack(grad_tokens),
        sums[:width],
        in_grad[:, :head_width],
        in_grad[:, head_width : 2 * head_width],
        in_grad[:, 2 * head_width : 3 * head_width],
        in_grad[:, 3 * head_width :],
        sums[2 * width :],
        output_grad,
        sums[width : 2 * width],
        pair_grad[:, :units_here],
        pair_grad[:, units_here:],
        down_grad,
    )


def solution(mesh):
    by_token = P(None, ("dp", "tensor"), None)
    by_column = P("dp", "tensor")
    by_row = P(("tensor", "dp"), None)
    weights = (by_column, by_column, by_column, by_column)
    return jax.shard_map(
        body,
        mesh=mesh,
        in_specs=(by_token, by_token, P(None, "dp"), P(None, "dp"), P())
        + weights
        + (P(), by_row, P(), by_column, by_column, by_row),
        out_specs=(by_token, by_token, P())
        + weights
        + (P(), by_row, P(), by_column, by_column, by_row),
        check_vma=False,
    )
```

```python
import functools
import jax
import jax.numpy as jnp
from jax import lax
from jax.experimental import pallas as pl
from jax.experimental.pallas import tpu as pltpu
from jax.sharding import PartitionSpec as P

EPS = 1e-05
F32 = jnp.float32
BF16 = jnp.bfloat16
LANES = 128
TILE = 256
BIG = 2.0**100


def three_parts(value):
    high = value.astype(BF16).astype(F32)
    rest = value - high
    middle = rest.astype(BF16).astype(F32)
    return high, middle, rest - middle


def lane_pick(array, lane, index):
    return jnp.sum(jnp.where(lane == index, array, 0.0), axis=1, keepdims=True)


def with_extras(data, keep, place, extras):
    total = jnp.where(keep, data, 0.0)
    for index, extra in enumerate(extras):
        total = jnp.where(place == index, extra, total)
    return total.astype(BF16)


def nt(left, right):
    return lax.dot_general(left, right, (((1,), (1,)), ((), ())), preferred_element_type=F32)


def nn(left, right):
    return lax.dot_general(left, right, (((1,), (0,)), ((), ())), preferred_element_type=F32)


def head_sides(head, heads, size, side_ref):
    length = side_ref.shape[0]
    lane = lax.broadcasted_iota(jnp.int32, (length, LANES), 1)
    half = lax.rem(head, 2)
    keep = (lane >= half * size) & (lane < (half + 1) * size)
    place = lane - (1 - half) * size
    place = jnp.where(keep, -1, place)
    side = side_ref[...]
    decay = lane_pick(side, lane, head)
    segment = side[:, heads : heads + 1]
    padded = 1.0 - side[:, heads + 1 : heads + 2]
    return lane, keep, place, decay, segment, padded


def key_extras(decay, segment, padded):
    high, middle, low = three_parts(-decay)
    return [high, middle, low, segment, 1.0 - segment, padded, 1.0, 1.0, 1.0]


def query_extras(segment, total):
    return [1.0, 1.0, 1.0, -BIG * (1.0 - segment), -BIG * segment, -BIG] + list(
        three_parts(-total)
    )


PADDED_AT = 5


def forward_kernel(heads, size, scale, q_ref, k_ref, v_ref, side_ref, o_ref, total_ref, ks_ref):
    head = pl.program_id(0)
    length = q_ref.shape[0]
    lane, keep, place, decay, segment, padded = head_sides(head, heads, size, side_ref)
    ks_ref[...] = with_extras(k_ref[...].astype(F32), keep, place, key_extras(decay, segment, padded))

    @pl.when(head == 0)
    def _():
        total_ref[...] = jnp.zeros_like(total_ref)

    row = lax.broadcasted_iota(jnp.int32, (TILE, TILE), 0)
    column = lax.broadcasted_iota(jnp.int32, (TILE, TILE), 1)
    for first in range(0, length, TILE):
        here = pl.ds(first, TILE)
        part = slice(first, first + TILE)
        full = with_extras(
            q_ref[here, :].astype(F32) * scale, keep[part], place[part],
            query_extras(segment[part], 0.0 * segment[part]),
        )
        bare = jnp.where(place[part] == PADDED_AT, 0.0, full.astype(F32)).astype(BF16)
        keys = ks_ref[here, :]
        near = jnp.where(
            column < row, nt(full, keys), jnp.where(column == row, nt(bare, keys), -BIG)
        )
        highest = jnp.max(near, axis=1, keepdims=True)
        if first:
            far = nt(full, ks_ref[pl.ds(0, first), :])
            highest = jnp.maximum(highest, jnp.max(far, axis=1, keepdims=True))
        near = jnp.exp(near - highest)
        below = jnp.sum(near, axis=1, keepdims=True)
        mixed = nn(near.astype(BF16), v_ref[here, :])
        if first:
            far = jnp.exp(far - highest)
            below = below + jnp.sum(far, axis=1, keepdims=True)
            mixed = mixed + nn(far.astype(BF16), v_ref[pl.ds(0, first), :])
        mixed = (mixed / below).astype(BF16)
        o_ref[here, :] = jnp.where(keep[part], mixed, o_ref[here, :])
        total_ref[here, :] = jnp.where(
            lane[part] == head, highest + jnp.log(below), total_ref[here, :]
        )


def backward_kernel(
    heads, size, scale, q_ref, k_ref, v_ref, side_ref, total_ref, o_ref, g_ref,
    dq_ref, dk_ref, dv_ref, dd_ref, ks_ref, kt_ref, vs_ref, ak_ref, av_ref, row_ref,
):
    head = pl.program_id(0)
    length = q_ref.shape[0]
    lane, keep, place, decay, segment, padded = head_sides(head, heads, size, side_ref)
    keys = with_extras(k_ref[...].astype(F32), keep, place, key_extras(decay, segment, padded))
    ks_ref[...] = keys
    kt_ref[...] = keys.astype(F32).T.astype(BF16)
    vs_ref[...] = with_extras(v_ref[...].astype(F32), keep, place, [1.0, 1.0, 1.0])
    total = lane_pick(total_ref[...], lane, head)
    grads = jnp.where(keep, g_ref[...].astype(F32), 0.0)
    delta = jnp.sum(grads * o_ref[...].astype(F32), axis=1, keepdims=True)
    ak_ref[...] = jnp.zeros_like(ak_ref)
    av_ref[...] = jnp.zeros_like(av_ref)

    @pl.when(head == 0)
    def _():
        dd_ref[...] = jnp.zeros_like(dd_ref)

    row = lax.broadcasted_iota(jnp.int32, (TILE, TILE), 0)
    column = lax.broadcasted_iota(jnp.int32, (TILE, TILE), 1)
    for first in range(0, length, TILE):
        here = pl.ds(first, TILE)
        part = slice(first, first + TILE)
        full = with_extras(
            q_ref[here, :].astype(F32) * scale, keep[part], place[part],
            query_extras(segment[part], total[part]),
        )
        bare = jnp.where(place[part] == PADDED_AT, 0.0, full.astype(F32)).astype(BF16)
        grad = with_extras(grads[part], keep[part], place[part], three_parts(-delta[part]))
        spans = [(first, TILE)] + ([(0, first)] if first else [])
        grad_query = None
        for start, count in spans:
            span = pl.ds(start, count)
            scores = nt(ks_ref[span, :], full)
            if start == first:
                scores = jnp.where(
                    row < column, scores, jnp.where(row == column, nt(ks_ref[span, :], bare), -BIG)
                )
            probs = jnp.exp(scores)
            low = (probs * nt(vs_ref[span, :], grad)).astype(BF16)
            av_ref[span, :] += nn(probs.astype(BF16), grad)
            ak_ref[span, :] += nn(low, full)
            piece = nn(kt_ref[:, span], low)
            grad_query = piece if grad_query is None else grad_query + piece
        grad_query = grad_query.T
        dq_ref[here, :] = jnp.where(keep[part], (grad_query * scale).astype(BF16), dq_ref[here, :])
        row_ref[here, :] = grad_query
    dk_ref[...] = jnp.where(keep, ak_ref[...].astype(BF16), dk_ref[...])
    dv_ref[...] = jnp.where(keep, av_ref[...].astype(BF16), dv_ref[...])
    by_row = lane_pick(row_ref[...], place, 6)
    by_column = lane_pick(ak_ref[...], place, 0)
    dd_ref[...] = jnp.where(lane == head, by_row - by_column, dd_ref[...])


def specs_for(length, size, heads):
    def pair(offset):
        return pl.BlockSpec((length, LANES), lambda h: (0, offset * heads * size // LANES + h // 2))

    return pair, pl.BlockSpec((length, LANES), lambda h: (0, 0))


def make_side(decay, segment, present):
    length, heads = decay.shape
    side = jnp.concatenate(
        (decay, segment[:, None].astype(F32), present[:, None].astype(F32)), axis=1
    )
    return jnp.pad(side, ((0, 0), (0, LANES - heads - 2)))


def attention_forward(projected, side, heads, size):
    length = projected.shape[0]
    pair, whole = specs_for(length, size, heads)
    return pl.pallas_call(
        functools.partial(forward_kernel, heads, size, size ** (-0.5)),
        grid=(heads,),
        in_specs=[pair(0), pair(1), pair(2), whole],
        out_specs=[pair(0), whole],
        out_shape=[
            jax.ShapeDtypeStruct((length, heads * size), BF16),
            jax.ShapeDtypeStruct((length, LANES), F32),
        ],
        scratch_shapes=[pltpu.VMEM((length, LANES), BF16)],
    )(projected, projected, projected, side)


def attention_backward(projected, side, total, mixed, grad_mixed, heads, size):
    length = projected.shape[0]
    pair, whole = specs_for(length, size, heads)
    flat = jax.ShapeDtypeStruct((length, heads * size), BF16)
    return pl.pallas_call(
        functools.partial(backward_kernel, heads, size, size ** (-0.5)),
        grid=(heads,),
        in_specs=[pair(0), pair(1), pair(2), whole, whole, pair(0), pair(0)],
        out_specs=[pair(0), pair(0), pair(0), whole],
        out_shape=[flat, flat, flat, jax.ShapeDtypeStruct((length, LANES), F32)],
        scratch_shapes=[
            pltpu.VMEM((length, LANES), BF16),
            pltpu.VMEM((LANES, length), BF16),
            pltpu.VMEM((length, LANES), BF16),
            pltpu.VMEM((length, LANES), F32),
            pltpu.VMEM((length, LANES), F32),
            pltpu.VMEM((length, LANES), F32),
        ],
    )(projected, projected, projected, side, total, mixed, grad_mixed)


def rms_forward(rows, gain):
    inverse = lax.rsqrt(jnp.mean(rows * rows, axis=-1, keepdims=True) + EPS)
    return (rows * inverse * gain, inverse)


def rms_backward(rows, inverse, gain, upstream):
    scaled = upstream * gain
    return inverse * scaled - rows * inverse**3 * jnp.mean(scaled * rows, axis=-1, keepdims=True)


def dot(left, right, left_dim, right_dim):
    return lax.dot_general(
        left, right, (((left_dim,), (right_dim,)), ((), ())), preferred_element_type=F32
    )


def after(value, *others):
    return lax.optimization_barrier((value,) + others)[0]


def sum_everywhere(value, axes):
    for axis in axes:
        size = lax.axis_size(axis)
        if size & (size - 1):
            value = lax.psum(value, axis)
            continue
        step = 1
        while step < size:
            value = value + lax.ppermute(value, axis, [(i, i ^ step) for i in range(size)])
            step *= 2
    return value


def body(
    tokens,
    cotangent,
    segment_ids,
    slot_mask,
    attention_gain,
    query_weight,
    key_weight,
    value_weight,
    forget_weight,
    forget_bias,
    output_weight,
    swiglu_gain,
    gate_weight,
    up_weight,
    down_weight,
):
    batches, here, width = tokens.shape
    ranks = lax.axis_size("tensor")
    groups = lax.axis_size("dp")
    length = here * ranks
    heads_here = forget_weight.shape[1]
    head_width = query_weight.shape[1]
    head_size = head_width // heads_here
    units_here = gate_weight.shape[1]
    units = units_here * ranks
    unit_piece = down_weight.shape[0]
    head_piece = output_weight.shape[0]
    rank = lax.axis_index("tensor")
    bias_here = lax.dynamic_slice_in_dim(forget_bias, rank * heads_here, heads_here)

    def shift(value, step):
        if step % ranks == 0:
            return value
        return lax.ppermute(value, "tensor", [(i, (i + step) % ranks) for i in range(ranks)])

    def pieces_of(value):
        return [shift(value, step) for step in range(ranks)]

    def row_block(value, owner):
        return lax.dynamic_slice_in_dim(value, (owner % ranks) * here, here, 0)

    def place_rows(blocks, owners):
        total = jnp.zeros((length,) + blocks[0].shape[1:], blocks[0].dtype)
        for block, owner in zip(blocks, owners):
            total = lax.dynamic_update_slice_in_dim(total, block, (owner % ranks) * here, 0)
        return total

    mixed_in = jnp.concatenate((query_weight, key_weight, value_weight, forget_weight), axis=1)
    full_in = lax.all_gather(mixed_in, "dp", axis=0, tiled=True)
    row_pieces = pieces_of(jnp.concatenate((output_weight, down_weight), axis=0))
    pair_pieces = pieces_of(
        after(jnp.concatenate((gate_weight, up_weight), axis=1), *row_pieces)
    )
    full_rows = lax.all_gather(jnp.stack(row_pieces), "dp", axis=0)
    full_output = full_rows[:, :, :head_piece].transpose(1, 0, 2, 3)
    full_output = full_output.reshape(ranks * head_width, width)
    full_down = full_rows[:, :, head_piece:].transpose(1, 0, 2, 3).reshape(units, width)

    pair_rows = jnp.concatenate(
        [piece[:, :units_here] for piece in pair_pieces]
        + [piece[:, units_here:] for piece in pair_pieces],
        axis=1,
    )
    full_pair = lax.all_gather(pair_rows, "dp", axis=0, tiled=True)

    rows = tokens.astype(F32)
    normed, inverse_one = rms_forward(rows, attention_gain)
    normed = normed.astype(BF16)
    saved = []
    mixed_parts = []
    previous = pair_pieces
    ready = None
    for batch in range(batches):
        normed_pieces = pieces_of(after(normed[batch], *previous[:2]))
        previous = normed_pieces
        if ready is not None:
            normed_pieces = lax.optimization_barrier((*normed_pieces, ready))[:ranks]
        normed_all = place_rows(normed_pieces, [rank - step + ranks for step in range(ranks)])
        projected = dot(normed_all, full_in[:, : 3 * head_width], 1, 0).astype(BF16)
        logits = dot(normed_all, full_in[:, 3 * head_width :], 1, 0) + bias_here
        decay = jnp.cumsum(jax.nn.log_sigmoid(logits), axis=0)
        side = make_side(decay, segment_ids[batch], slot_mask[batch])
        mixed, total = attention_forward(projected, side, heads_here, head_size)
        ready = total
        mixed_parts.append(
            jnp.concatenate(
                [shift(row_block(mixed, rank + step), step) for step in range(ranks)], axis=1
            )
        )
        saved.append((normed_all, projected, logits, side, total, mixed))

    mixed_here = jnp.concatenate(mixed_parts, axis=0)
    rows = rows.reshape(batches * here, width)
    upstream = cotangent.reshape(batches * here, width)
    hidden_state = rows + dot(mixed_here, full_output, 1, 0)
    normed_two, inverse_two = rms_forward(hidden_state, swiglu_gain)
    normed_two = normed_two.astype(BF16)
    both = dot(normed_two, full_pair, 1, 0)
    gate, upper = both[:, :units], both[:, units:]
    sigmoid_gate = jax.nn.sigmoid(gate)
    inner = (gate * sigmoid_gate * upper).astype(BF16)

    def scatter(value):
        return lax.psum_scatter(value, "dp", scatter_dimension=0, tiled=True)

    def settle(blocks):
        pieces = [shift(blocks[step], ranks - step) for step in range(ranks)]
        total = pieces[0].astype(F32)
        for piece in pieces[1:]:
            total = total + piece.astype(F32)
        return total, pieces

    by_shard = inner.reshape(-1, ranks, groups, unit_piece).transpose(0, 2, 1, 3)
    down_partial = dot(by_shard.reshape(inner.shape), upstream, 0, 0).astype(BF16)
    down_rows = scatter(down_partial)
    upstream_late = after(upstream, down_partial)
    grad_inner = dot(upstream_late, full_down, 1, 1)
    grad_both = jnp.concatenate(
        (
            (grad_inner * upper * sigmoid_gate * (1.0 + gate * (1.0 - sigmoid_gate))).astype(BF16),
            (grad_inner * gate * sigmoid_gate).astype(BF16),
        ),
        axis=1,
    )
    grad_normed_two = dot(grad_both, full_pair, 1, 1)
    gain_two = jnp.sum(grad_normed_two * hidden_state * inverse_two, axis=0)
    grad_hidden = upstream.astype(F32) + rms_backward(
        hidden_state, inverse_two, swiglu_gain, grad_normed_two
    )
    branch = grad_hidden.astype(BF16)
    grad_mixed_here = dot(branch, full_output, 1, 1).astype(BF16)
    pair_partial = dot(after(normed_two, grad_mixed_here), grad_both, 0, 0).astype(BF16)
    pair_grad = scatter(after(pair_partial, down_rows))
    down_rows = down_rows.reshape(ranks, unit_piece, width)
    down_grad, _ = settle([down_rows[step] for step in range(ranks)])
    inner_late, branch_late = lax.optimization_barrier((inner, branch, pair_partial))[:2]
    layer_out = (hidden_state + dot(inner_late, full_down, 1, 0)).astype(BF16)
    output_partial = dot(mixed_here, branch_late, 0, 0).astype(BF16)
    output_partial = output_partial.reshape(ranks, groups, head_piece, width)
    output_partial = output_partial.transpose(1, 0, 2, 3).reshape(ranks * head_width, width)

    projected_grads = []
    arrivals = []
    bias_grad = jnp.zeros((heads_here,), F32)
    gain_one = jnp.zeros((width,), F32)
    grad_tokens = []
    for batch in range(batches):
        normed_all, projected, logits, side, total, mixed = saved[batch]
        part = grad_mixed_here[batch * here : (batch + 1) * here]
        blocks = [
            shift(part[:, step * head_width : (step + 1) * head_width], ranks - step)
            for step in range(ranks)
        ]
        grad_mixed = place_rows(blocks, [rank + step for step in range(ranks)])
        if batch + 1 == batches:
            grad_mixed = after(grad_mixed, down_grad, partial)
        grad_queries, grad_keys, grad_values, grad_decay = attention_backward(
            projected, side, total, mixed, grad_mixed, heads_here, head_size
        )
        carried = lax.cumsum(grad_decay[:, :heads_here], axis=0, reverse=True)
        grad_logits = (carried * jax.nn.sigmoid(-logits)).astype(BF16)
        projected_grad = jnp.concatenate(
            (grad_queries, grad_keys, grad_values, grad_logits), axis=1
        )
        projected_grads.append(projected_grad)
        bias_grad = bias_grad + jnp.sum(grad_logits.astype(F32), axis=0)
        partial = dot(projected_grad, full_in, 1, 1).astype(BF16)
        arrivals.append([shift(row_block(partial, rank + step), step) for step in range(ranks)])
    in_partial = dot(
        jnp.concatenate([item[0] for item in saved], axis=0),
        after(jnp.concatenate(projected_grads, axis=0), partial, *arrivals[0]),
        0,
        0,
    ).astype(BF16)
    arrivals[-1] = lax.optimization_barrier((*arrivals[-1], in_partial))[:ranks]
    for batch in range(batches):
        grad_normed = arrivals[batch][0].astype(F32)
        for piece in arrivals[batch][1:]:
            grad_normed = grad_normed + piece.astype(F32)
        own = rows[batch * here : (batch + 1) * here]
        gain_one = gain_one + jnp.sum(grad_normed * own * inverse_one[batch], axis=0)
        grad_tokens.append(
            grad_hidden[batch * here : (batch + 1) * here]
            + rms_backward(own, inverse_one[batch], attention_gain, grad_normed)
        )
    last = scatter(after(jnp.concatenate((output_partial, in_partial), axis=1), pair_grad))
    in_grad = last[:, width:].astype(F32)

    columns = [pair_grad[:, i * units_here : (i + 1) * units_here] for i in range(2 * ranks)]
    pair_grad, pair_pieces = settle(
        [jnp.concatenate((columns[i], columns[ranks + i]), axis=1) for i in range(ranks)]
    )
    output_rows = last[:, :width].reshape(ranks, head_piece, width)
    output_grad, _ = settle([output_rows[step] for step in range(ranks)])
    bias_full = lax.dynamic_update_slice_in_dim(
        jnp.zeros(forget_bias.shape, F32), bias_grad, rank * heads_here, 0
    )
    sums = after(jnp.concatenate((gain_one, gain_two, bias_full)), pair_pieces[1])
    sums = sum_everywhere(sums, ("dp", "tensor"))
    return (
        layer_out.reshape(batches, here, width),
        jnp.stack(grad_tokens),
        sums[:width],
        in_grad[:, :head_width],
        in_grad[:, head_width : 2 * head_width],
        in_grad[:, 2 * head_width : 3 * head_width],
        in_grad[:, 3 * head_width :],
        sums[2 * width :],
        output_grad,
        sums[width : 2 * width],
        pair_grad[:, :units_here],
        pair_grad[:, units_here:],
        down_grad,
    )


def solution(mesh):
    by_token = P(None, ("dp", "tensor"), None)
    by_column = P("dp", "tensor")
    by_row = P(("tensor", "dp"), None)
    weights = (by_column, by_column, by_column, by_column)
    return jax.shard_map(
        body,
        mesh=mesh,
        in_specs=(by_token, by_token, P(None, "dp"), P(None, "dp"), P())
        + weights
        + (P(), by_row, P(), by_column, by_column, by_row),
        out_specs=(by_token, by_token, P())
        + weights
        + (P(), by_row, P(), by_column, by_column, by_row),
        check_vma=False,
    )
```

```python
import functools
import jax
import jax.numpy as jnp
from jax import lax
from jax.experimental import pallas as pl
from jax.experimental.pallas import tpu as pltpu
from jax.sharding import PartitionSpec as P


EPS = 1e-05
F32 = jnp.float32
BF16 = jnp.bfloat16
LANES = 128
TILE = 256
BIG = 2.0**100


def three_parts(value):
    high = value.astype(BF16).astype(F32)
    rest = value - high
    middle = rest.astype(BF16).astype(F32)
    return high, middle, rest - middle


def lane_pick(array, lane, index):
    return jnp.sum(jnp.where(lane == index, array, 0.0), axis=1, keepdims=True)


def with_extras(data, keep, place, extras):
    total = jnp.where(keep, data, 0.0)
    for index, extra in enumerate(extras):
        total = jnp.where(place == index, extra, total)
    return total.astype(BF16)


def nt(left, right):
    return lax.dot_general(left, right, (((1,), (1,)), ((), ())), preferred_element_type=F32)


def nn(left, right):
    return lax.dot_general(left, right, (((1,), (0,)), ((), ())), preferred_element_type=F32)


def head_sides(head, heads, size, side_ref):
    length = side_ref.shape[0]
    lane = lax.broadcasted_iota(jnp.int32, (length, LANES), 1)
    half = lax.rem(head, 2)
    keep = (lane >= half * size) & (lane < (half + 1) * size)
    place = lane - (1 - half) * size
    place = jnp.where(keep, -1, place)
    side = side_ref[...]
    decay = lane_pick(side, lane, head)
    segment = side[:, heads : heads + 1]
    padded = 1.0 - side[:, heads + 1 : heads + 2]
    return lane, keep, place, decay, segment, padded


def key_extras(decay, segment, padded):
    high, middle, low = three_parts(-decay)
    return [high, middle, low, segment, 1.0 - segment, padded, 1.0, 1.0, 1.0]


def query_extras(segment, total):
    return [1.0, 1.0, 1.0, -BIG * (1.0 - segment), -BIG * segment, -BIG] + list(
        three_parts(-total)
    )


PADDED_AT = 5


def forward_kernel(heads, size, scale, q_ref, k_ref, v_ref, side_ref, o_ref, total_ref, ks_ref):
    head = pl.program_id(0)
    length = q_ref.shape[0]
    lane, keep, place, decay, segment, padded = head_sides(head, heads, size, side_ref)
    ks_ref[...] = with_extras(k_ref[...].astype(F32), keep, place, key_extras(decay, segment, padded))

    @pl.when(head == 0)
    def _():
        total_ref[...] = jnp.zeros_like(total_ref)

    row = lax.broadcasted_iota(jnp.int32, (TILE, TILE), 0)
    column = lax.broadcasted_iota(jnp.int32, (TILE, TILE), 1)
    for first in range(0, length, TILE):
        here = pl.ds(first, TILE)
        part = slice(first, first + TILE)
        full = with_extras(
            q_ref[here, :].astype(F32) * scale, keep[part], place[part],
            query_extras(segment[part], 0.0 * segment[part]),
        )
        bare = jnp.where(place[part] == PADDED_AT, 0.0, full.astype(F32)).astype(BF16)
        keys = ks_ref[here, :]
        near = jnp.where(
            column < row, nt(full, keys), jnp.where(column == row, nt(bare, keys), -BIG)
        )
        highest = jnp.max(near, axis=1, keepdims=True)
        if first:
            far = nt(full, ks_ref[pl.ds(0, first), :])
            highest = jnp.maximum(highest, jnp.max(far, axis=1, keepdims=True))
        near = jnp.exp(near - highest)
        below = jnp.sum(near, axis=1, keepdims=True)
        mixed = nn(near.astype(BF16), v_ref[here, :])
        if first:
            far = jnp.exp(far - highest)
            below = below + jnp.sum(far, axis=1, keepdims=True)
            mixed = mixed + nn(far.astype(BF16), v_ref[pl.ds(0, first), :])
        mixed = (mixed / below).astype(BF16)
        o_ref[here, :] = jnp.where(keep[part], mixed, o_ref[here, :])
        total_ref[here, :] = jnp.where(
            lane[part] == head, highest + jnp.log(below), total_ref[here, :]
        )


def backward_kernel(
    heads, size, scale, q_ref, k_ref, v_ref, side_ref, total_ref, o_ref, g_ref,
    dq_ref, dk_ref, dv_ref, dd_ref, ks_ref, kt_ref, vs_ref, ak_ref, av_ref, row_ref,
):
    head = pl.program_id(0)
    length = q_ref.shape[0]
    lane, keep, place, decay, segment, padded = head_sides(head, heads, size, side_ref)
    keys = with_extras(k_ref[...].astype(F32), keep, place, key_extras(decay, segment, padded))
    ks_ref[...] = keys
    kt_ref[...] = keys.astype(F32).T.astype(BF16)
    vs_ref[...] = with_extras(v_ref[...].astype(F32), keep, place, [1.0, 1.0, 1.0])
    total = lane_pick(total_ref[...], lane, head)
    grads = jnp.where(keep, g_ref[...].astype(F32), 0.0)
    delta = jnp.sum(grads * o_ref[...].astype(F32), axis=1, keepdims=True)
    ak_ref[...] = jnp.zeros_like(ak_ref)
    av_ref[...] = jnp.zeros_like(av_ref)

    @pl.when(head == 0)
    def _():
        dd_ref[...] = jnp.zeros_like(dd_ref)

    row = lax.broadcasted_iota(jnp.int32, (TILE, TILE), 0)
    column = lax.broadcasted_iota(jnp.int32, (TILE, TILE), 1)
    for first in range(0, length, TILE):
        here = pl.ds(first, TILE)
        part = slice(first, first + TILE)
        full = with_extras(
            q_ref[here, :].astype(F32) * scale, keep[part], place[part],
            query_extras(segment[part], total[part]),
        )
        bare = jnp.where(place[part] == PADDED_AT, 0.0, full.astype(F32)).astype(BF16)
        grad = with_extras(grads[part], keep[part], place[part], three_parts(-delta[part]))
        spans = [(first, TILE)] + ([(0, first)] if first else [])
        grad_query = None
        for start, count in spans:
            span = pl.ds(start, count)
            scores = nt(ks_ref[span, :], full)
            if start == first:
                scores = jnp.where(
                    row < column, scores, jnp.where(row == column, nt(ks_ref[span, :], bare), -BIG)
                )
            probs = jnp.exp(scores)
            low = (probs * nt(vs_ref[span, :], grad)).astype(BF16)
            av_ref[span, :] += nn(probs.astype(BF16), grad)
            ak_ref[span, :] += nn(low, full)
            piece = nn(kt_ref[:, span], low)
            grad_query = piece if grad_query is None else grad_query + piece
        grad_query = grad_query.T
        dq_ref[here, :] = jnp.where(keep[part], (grad_query * scale).astype(BF16), dq_ref[here, :])
        row_ref[here, :] = grad_query
    dk_ref[...] = jnp.where(keep, ak_ref[...].astype(BF16), dk_ref[...])
    dv_ref[...] = jnp.where(keep, av_ref[...].astype(BF16), dv_ref[...])
    by_row = lane_pick(row_ref[...], place, 6)
    by_column = lane_pick(ak_ref[...], place, 0)
    dd_ref[...] = jnp.where(lane == head, by_row - by_column, dd_ref[...])


def specs_for(length, size, heads):
    def pair(offset):
        return pl.BlockSpec((length, LANES), lambda h: (0, offset * heads * size // LANES + h // 2))

    return pair, pl.BlockSpec((length, LANES), lambda h: (0, 0))


def make_side(decay, segment, present):
    _, heads = decay.shape
    side = jnp.concatenate(
        (decay, segment[:, None].astype(F32), present[:, None].astype(F32)), axis=1
    )
    return jnp.pad(side, ((0, 0), (0, LANES - heads - 2)))


def attention_forward(projected, side, heads, size):
    length = projected.shape[0]
    pair, whole = specs_for(length, size, heads)
    return pl.pallas_call(
        functools.partial(forward_kernel, heads, size, size ** (-0.5)),
        grid=(heads,),
        in_specs=[pair(0), pair(1), pair(2), whole],
        out_specs=[pair(0), whole],
        out_shape=[
            jax.ShapeDtypeStruct((length, heads * size), BF16),
            jax.ShapeDtypeStruct((length, LANES), F32),
        ],
        scratch_shapes=[pltpu.VMEM((length, LANES), BF16)],
    )(projected, projected, projected, side)


def attention_backward(projected, side, total, mixed, grad_mixed, heads, size):
    length = projected.shape[0]
    pair, whole = specs_for(length, size, heads)
    flat = jax.ShapeDtypeStruct((length, heads * size), BF16)
    return pl.pallas_call(
        functools.partial(backward_kernel, heads, size, size ** (-0.5)),
        grid=(heads,),
        in_specs=[pair(0), pair(1), pair(2), whole, whole, pair(0), pair(0)],
        out_specs=[pair(0), pair(0), pair(0), whole],
        out_shape=[flat, flat, flat, jax.ShapeDtypeStruct((length, LANES), F32)],
        scratch_shapes=[
            pltpu.VMEM((length, LANES), BF16),
            pltpu.VMEM((LANES, length), BF16),
            pltpu.VMEM((length, LANES), BF16),
            pltpu.VMEM((length, LANES), F32),
            pltpu.VMEM((length, LANES), F32),
            pltpu.VMEM((length, LANES), F32),
        ],
    )(projected, projected, projected, side, total, mixed, grad_mixed)


def rms_forward(rows, gain):
    inverse = lax.rsqrt(jnp.mean(rows * rows, axis=-1, keepdims=True) + EPS)
    return (rows * inverse * gain, inverse)


def rms_backward(rows, inverse, gain, upstream):
    scaled = upstream * gain
    return inverse * scaled - rows * inverse**3 * jnp.mean(scaled * rows, axis=-1, keepdims=True)


def dot(left, right, left_dim, right_dim):
    return lax.dot_general(
        left, right, (((left_dim,), (right_dim,)), ((), ())), preferred_element_type=F32
    )


def after(value, *others):
    return lax.optimization_barrier((value,) + others)[0]


def sum_everywhere(value, axes):
    for axis in axes:
        size = lax.axis_size(axis)
        if size & (size - 1):
            value = lax.psum(value, axis)
            continue
        step = 1
        while step < size:
            value = value + lax.ppermute(value, axis, [(i, i ^ step) for i in range(size)])
            step *= 2
    return value


def body(
    tokens,
    cotangent,
    segment_ids,
    slot_mask,
    attention_gain,
    query_weight,
    key_weight,
    value_weight,
    forget_weight,
    forget_bias,
    output_weight,
    swiglu_gain,
    gate_weight,
    up_weight,
    down_weight,
):
    batches, here, width = tokens.shape
    ranks = lax.axis_size("tensor")
    groups = lax.axis_size("dp")
    length = here * ranks
    heads_here = forget_weight.shape[1]
    head_width = query_weight.shape[1]
    head_size = head_width // heads_here
    units_here = gate_weight.shape[1]
    units = units_here * ranks
    unit_piece = down_weight.shape[0]
    head_piece = output_weight.shape[0]
    rank = lax.axis_index("tensor")
    bias_here = lax.dynamic_slice_in_dim(forget_bias, rank * heads_here, heads_here)

    def shift(value, step):
        if step % ranks == 0:
            return value
        return lax.ppermute(value, "tensor", [(i, (i + step) % ranks) for i in range(ranks)])

    def pieces_of(value):
        return [shift(value, step) for step in range(ranks)]

    def row_block(value, owner):
        return lax.dynamic_slice_in_dim(value, (owner % ranks) * here, here, 0)

    def place_rows(blocks, owners):
        total = jnp.zeros((length,) + blocks[0].shape[1:], blocks[0].dtype)
        for block, owner in zip(blocks, owners):
            total = lax.dynamic_update_slice_in_dim(total, block, (owner % ranks) * here, 0)
        return total

    mixed_in = jnp.concatenate((query_weight, key_weight, value_weight, forget_weight), axis=1)
    full_in = lax.all_gather(mixed_in, "dp", axis=0, tiled=True)
    row_pieces = pieces_of(jnp.concatenate((output_weight, down_weight), axis=0))
    pair_pieces = pieces_of(
        after(jnp.concatenate((gate_weight, up_weight), axis=1), *row_pieces)
    )
    full_rows = lax.all_gather(jnp.stack(row_pieces), "dp", axis=0)
    full_output = full_rows[:, :, :head_piece].transpose(1, 0, 2, 3)
    full_output = full_output.reshape(ranks * head_width, width)
    full_down = full_rows[:, :, head_piece:].transpose(1, 0, 2, 3).reshape(units, width)

    pair_rows = jnp.concatenate(
        [piece[:, :units_here] for piece in pair_pieces]
        + [piece[:, units_here:] for piece in pair_pieces],
        axis=1,
    )
    full_pair = lax.all_gather(pair_rows, "dp", axis=0, tiled=True)

    rows = tokens.astype(F32)
    normed, inverse_one = rms_forward(rows, attention_gain)
    normed = normed.astype(BF16)
    saved = []
    mixed_parts = []
    previous = pair_pieces
    ready = None
    for batch in range(batches):
        normed_pieces = pieces_of(after(normed[batch], *previous[:2]))
        previous = normed_pieces
        if ready is not None:
            normed_pieces = lax.optimization_barrier((*normed_pieces, ready))[:ranks]
        normed_all = place_rows(normed_pieces, [rank - step + ranks for step in range(ranks)])
        projected = dot(normed_all, full_in[:, : 3 * head_width], 1, 0).astype(BF16)
        logits = dot(normed_all, full_in[:, 3 * head_width :], 1, 0) + bias_here
        decay = jnp.cumsum(jax.nn.log_sigmoid(logits), axis=0)
        side = make_side(decay, segment_ids[batch], slot_mask[batch])
        mixed, total = attention_forward(projected, side, heads_here, head_size)
        ready = total
        mixed_pieces = [shift(row_block(mixed, rank + step), step) for step in range(ranks)]
        mixed_parts.append(jnp.concatenate(mixed_pieces, axis=1))
        saved.append((normed_all, projected, logits, side, total, mixed))

    rows = [tokens[batch].astype(F32) for batch in range(batches)]
    forward = []
    for batch in range(batches):
        hidden_state = rows[batch] + dot(mixed_parts[batch], full_output, 1, 0)
        normed_two, inverse_two = rms_forward(hidden_state, swiglu_gain)
        normed_two = normed_two.astype(BF16)
        both = dot(normed_two, full_pair, 1, 0)
        gate, upper = both[:, :units], both[:, units:]
        sigmoid_gate = jax.nn.sigmoid(gate)
        inner = (gate * sigmoid_gate * upper).astype(BF16)
        forward.append((hidden_state, normed_two, inverse_two, gate, upper, sigmoid_gate, inner))

    def scatter(value):
        return lax.psum_scatter(value, "dp", scatter_dimension=0, tiled=True)

    def settle(blocks):
        pieces = [shift(blocks[step], ranks - step) for step in range(ranks)]
        total = pieces[0].astype(F32)
        for piece in pieces[1:]:
            total = total + piece.astype(F32)
        return total

    mixed_here = jnp.concatenate(mixed_parts, axis=0)
    inner = jnp.concatenate([item[-1] for item in forward], axis=0)
    upstream = cotangent.reshape(batches * here, width)
    down_partial = dot(inner, upstream, 0, 0).astype(BF16)
    down_rows = lax.psum_scatter(
        down_partial.reshape(ranks, groups * unit_piece, width),
        "dp",
        scatter_dimension=1,
        tiled=True,
    )

    gain_two = jnp.zeros((width,), F32)
    grad_both_parts = []
    grad_hidden_parts = []
    branch_parts = []
    grad_mixed_parts = []
    previous = down_partial
    for batch in range(batches):
        hidden_state, _, inverse_two, gate, upper, sigmoid_gate, _ = forward[batch]
        late = after(cotangent[batch], previous)
        grad_inner = dot(late, full_down, 1, 1)
        grad_both = jnp.concatenate(
            (
                (grad_inner * upper * sigmoid_gate * (1.0 + gate * (1.0 - sigmoid_gate))).astype(
                    BF16
                ),
                (grad_inner * gate * sigmoid_gate).astype(BF16),
            ),
            axis=1,
        )
        grad_both_parts.append(grad_both)
        if batch + 1 == batches:
            normed_two = jnp.concatenate([item[1] for item in forward], axis=0)
            pair_partial = dot(
                normed_two, jnp.concatenate(grad_both_parts, axis=0), 0, 0
            ).astype(BF16)
            grad_both = after(grad_both, pair_partial)
        grad_normed_two = dot(grad_both, full_pair, 1, 1)
        gain_two = gain_two + jnp.sum(grad_normed_two * hidden_state * inverse_two, axis=0)
        grad_hidden = late.astype(F32) + rms_backward(
            hidden_state, inverse_two, swiglu_gain, grad_normed_two
        )
        branch = grad_hidden.astype(BF16)
        grad_mixed_here = dot(branch, full_output, 1, 1).astype(BF16)
        previous = grad_mixed_here
        grad_hidden_parts.append(grad_hidden)
        branch_parts.append(branch)
        grad_mixed_parts.append(grad_mixed_here)
    pair_grad = scatter(after(pair_partial, down_rows))
    down_grad = settle([down_rows[step] for step in range(ranks)])
    inner_late, branch_late = lax.optimization_barrier(
        (inner, jnp.concatenate(branch_parts, axis=0), pair_partial)
    )[:2]
    hidden_state = jnp.concatenate([item[0] for item in forward], axis=0)
    layer_out = (hidden_state + dot(inner_late, full_down, 1, 0)).astype(BF16)
    output_partial = dot(mixed_here, branch_late, 0, 0).astype(BF16)
    output_partial = output_partial.reshape(ranks, groups, head_piece, width)
    output_partial = output_partial.transpose(1, 0, 2, 3).reshape(ranks * head_width, width)

    projected_grads = []
    arrivals = []
    partial = pair_partial
    bias_grad = jnp.zeros((heads_here,), F32)
    gain_one = jnp.zeros((width,), F32)
    grad_tokens = []
    for batch in range(batches):
        normed_all, projected, logits, side, total, mixed = saved[batch]
        part = grad_mixed_parts[batch]
        blocks = [
            shift(part[:, step * head_width : (step + 1) * head_width], ranks - step)
            for step in range(ranks)
        ]
        grad_mixed = place_rows(blocks, [rank + step for step in range(ranks)])
        grad_mixed = after(grad_mixed, partial)
        grad_queries, grad_keys, grad_values, grad_decay = attention_backward(
            projected, side, total, mixed, grad_mixed, heads_here, head_size
        )
        carried = lax.cumsum(grad_decay[:, :heads_here], axis=0, reverse=True)
        grad_logits = (carried * jax.nn.sigmoid(-logits)).astype(BF16)
        projected_grad = jnp.concatenate(
            (grad_queries, grad_keys, grad_values, grad_logits), axis=1
        )
        projected_grads.append(projected_grad)
        bias_grad = bias_grad + jnp.sum(grad_logits.astype(F32), axis=0)
        partial = dot(projected_grad, full_in, 1, 1).astype(BF16)
        arrivals.append(
            [shift(row_block(partial, rank + step), step) for step in range(ranks)]
        )
    late_grads = list(projected_grads)
    late_grads[-1] = after(late_grads[-1], partial)
    in_partial = sum(
        dot(item[0], gradient, 0, 0) for item, gradient in zip(saved, late_grads)
    ).astype(BF16)
    arrivals[-1] = lax.optimization_barrier((*arrivals[-1], in_partial))[:ranks]
    for batch in range(batches):
        grad_normed = arrivals[batch][0].astype(F32)
        for piece in arrivals[batch][1:]:
            grad_normed = grad_normed + piece.astype(F32)
        own = rows[batch]
        gain_one = gain_one + jnp.sum(grad_normed * own * inverse_one[batch], axis=0)
        grad_tokens.append(
            grad_hidden_parts[batch]
            + rms_backward(own, inverse_one[batch], attention_gain, grad_normed)
        )
    last = scatter(after(jnp.concatenate((output_partial, in_partial), axis=1), pair_grad))
    in_grad = last[:, width:].astype(F32)

    columns = [pair_grad[:, i * units_here : (i + 1) * units_here] for i in range(2 * ranks)]
    pair_grad = settle(
        [jnp.concatenate((columns[i], columns[ranks + i]), axis=1) for i in range(ranks)]
    )
    output_rows = last[:, :width].reshape(ranks, head_piece, width)
    output_grad = settle([output_rows[step] for step in range(ranks)])
    bias_full = lax.dynamic_update_slice_in_dim(
        jnp.zeros(forget_bias.shape, F32), bias_grad, rank * heads_here, 0
    )
    sums = jnp.concatenate((gain_one, gain_two, bias_full))
    sums = sum_everywhere(sums, ("dp", "tensor"))
    return (
        layer_out.reshape(batches, here, width),
        jnp.stack(grad_tokens),
        sums[:width],
        in_grad[:, :head_width],
        in_grad[:, head_width : 2 * head_width],
        in_grad[:, 2 * head_width : 3 * head_width],
        in_grad[:, 3 * head_width :],
        sums[2 * width :],
        output_grad,
        sums[width : 2 * width],
        pair_grad[:, :units_here],
        pair_grad[:, units_here:],
        down_grad,
    )


def solution(mesh):
    by_token = P(None, ("dp", "tensor"), None)
    by_column = P("dp", "tensor")
    by_row = P(("tensor", "dp"), None)
    weights = (by_column, by_column, by_column, by_column)

    return jax.shard_map(
        body,
        mesh=mesh,
        in_specs=(by_token, by_token, P(None, "dp"), P(None, "dp"), P())
        + weights
        + (P(), by_row, P(), by_column, by_column, by_row),
        out_specs=(by_token, by_token, P())
        + weights
        + (P(), by_row, P(), by_column, by_column, by_row),
        check_vma=False,
    )
```
